32 devices in a mesh: dp: 8 (over y, x, core), gz: 4 (over z).
Axes of the slice: x: 2, y: 2, z: 4, core: 2. Of those that a mesh axis runs over, the one named last changes fastest.
Arguments:
- volume: bfloat16 [8, 8, 32, 32, 128], P('dp', 'gz'), may hold values from -6 to 6
- cotangent: bfloat16 [8, 4, 16, 16, 256], P('dp', 'gz'), may hold values from -48 to 48
- weight: float32 [8, 27, 128, 256], P('dp'), may hold values from -6 to 6
- bias: float32 [8, 256], P('dp'), may hold values from -3 to 3
- exponent: int32 [4], replicated, may hold values from 0 to 2
Outputs:
- new_weight: float32 [8, 27, 128, 256], P('dp')
- new_bias: float32 [8, 256], P('dp')
- input_grad: bfloat16 [8, 8, 32, 32, 128], P('dp', 'gz')
The draws below stay inside these ranges and needn't reach their ends.
All inputs are finite; a program needn't handle non-finite values.
Results may differ from the reference program's by a relative error of at most 0.0062.
Values may be sent and summed in bfloat16 or wider, within the bound.
No kernel may reach another device: no remote copies, remote signals or barrier semaphores. Data moves between devices by JAX's collectives and lax.ppermute only.
A program may use at most 128 MiB of HBM per device.

```python
import math
import jax
import jax.numpy as jnp
from jax import lax

CIN = 128
COUT = 256
TAPS = 27
PLANE = 32
ROUNDS = 4
VZ = 8
REPLICAS = 8
LOG_DP = 3


def set_ends(drawn, key, least, high):
    dims = drawn.shape
    index_at = [jax.random.randint(jax.random.fold_in(key, axis), (), 0, dims[axis]) for axis in range(len(dims))]
    drawn = drawn.at[tuple(index_at)].set(least)
    longest = dims.index(max(dims))
    index_at[longest] = (index_at[longest] + 1) % dims[longest]
    return drawn.at[tuple(index_at)].set(high)


def steps_of(stream_key, shape, cuts, low, top_value):
    def one(dim, parts):
        draws = jax.random.uniform(jax.random.fold_in(jax.random.fold_in(stream_key, 6), dim), (parts,), jnp.float32, low / len(cuts), top_value / len(cuts))
        return jnp.repeat(jnp.exp(draws), shape[dim] // parts).reshape((-1,) + (1,) * (len(shape) - dim - 1))

    level = one(*cuts[0])
    for cut in cuts[1:]:
        level = level * one(*cut)
    return level


def gaussian(rng, dims, scale, most, cuts=(), held_as=jnp.bfloat16):
    entries = scale * jax.random.normal(rng, dims, jnp.float32)
    if cuts:
        entries = entries * steps_of(rng, dims, cuts, -0.22, 0.18)
    return jnp.clip(entries, -most, most).astype(held_as)


def setup_inputs(seed: int = 0) -> dict:
    splits = jax.random.split(jax.random.key(seed), 6)
    volume = gaussian(splits[0], (REPLICAS, VZ, PLANE, PLANE, CIN), 1.0, 6.0, ((0, 8), (1, 4)))
    cotangent = gaussian(splits[1], (REPLICAS, VZ // 2, PLANE // 2, PLANE // 2, COUT), 8.0, 48.0, ((0, 8), (1, 4)))
    weight = gaussian(splits[2], (REPLICAS, TAPS, CIN, COUT), 1.0, 6.0, ((0, 8),), jnp.float32)
    bias = gaussian(splits[3], (REPLICAS, COUT), 0.5, 3.0, ((0, 8),), jnp.float32)
    exponent = set_ends(jax.random.randint(splits[4], (ROUNDS,), 0, LOG_DP), jax.random.fold_in(splits[4], 1), 0, LOG_DP - 1).astype(jnp.int32)
    return {"volume": volume, "cotangent": cotangent, "weight": weight, "bias": bias, "exponent": exponent}


learning_rate = 0.5
cubic = 0.044715

def gelu_slope(values):
    factor = math.sqrt(2.0 / math.pi)
    inner_arg = factor * (values + cubic * values * values * values)
    tangent = jnp.tanh(inner_arg)
    return 0.5 * (1.0 + tangent) + 0.5 * values * (1.0 - tangent * tangent) * factor * (1.0 + 3.0 * cubic * values * values)

def plane_patches(padded, plane_width):
    return jnp.concatenate([padded[:, row_off:row_off + plane_width, col_off:col_off + plane_width, :] for row_off in range(3) for col_off in range(3)], axis=3)

def forward_terms(padded, low_three, planes, plane_width):
    patches = plane_patches(padded, plane_width)
    cell_count = planes * plane_width * plane_width
    preact = jnp.zeros((cell_count, low_three.shape[2]), jnp.float32)
    for depth_off in range(3):
        flat = patches[depth_off:depth_off + planes].reshape(cell_count, -1)
        preact = preact + jnp.dot(flat, low_three[depth_off], preferred_element_type=jnp.float32)
    return (patches, preact)

def weight_terms(patches, grad_pre, planes, plane_width, in_channels):
    cell_count = planes * plane_width * plane_width
    blocks = []
    for depth_off in range(3):
        flat = patches[depth_off:depth_off + planes].reshape(cell_count, -1)
        blocks.append(jnp.dot(flat.T, grad_pre, preferred_element_type=jnp.float32))
    stacked = jnp.stack(blocks, axis=0)
    return stacked.reshape(27, in_channels, grad_pre.shape[1])

def input_terms(grad_pad, low_weight, planes, plane_width):
    cell_count = planes * plane_width * plane_width
    accumulated = jnp.zeros((cell_count, low_weight.shape[1]), jnp.float32)
    for depth_off in range(3):
        for row_off in range(3):
            pieces = jnp.concatenate([grad_pad[2 - depth_off:2 - depth_off + planes, 2 - row_off:2 - row_off + plane_width, 2 - col_off:2 - col_off + plane_width, :] for col_off in range(3)], axis=3)
            kernel_block = jnp.concatenate([low_weight[depth_off * 9 + row_off * 3 + col_off].T for col_off in range(3)], axis=0)
            accumulated = accumulated + jnp.dot(pieces.reshape(cell_count, -1), kernel_block, preferred_element_type=jnp.float32)
    return accumulated

def spread_cotangent(cotangent, planes, plane_width, out_channels):
    widened = jnp.broadcast_to(cotangent.astype(jnp.float32)[:, None, :, None, :, None, :], (planes // 2, 2, plane_width // 2, 2, plane_width // 2, 2, out_channels))
    return widened.reshape(planes * plane_width * plane_width, out_channels)

def replica_step(packed):
    volume, cotangent, weight, bias = packed
    planes, plane_width, _, in_channels = volume.shape
    out_channels = weight.shape[2]
    scaling = (weight.shape[0] * in_channels) ** (-0.5)
    low_weight = (scaling * weight).astype(jnp.bfloat16)
    low_three = low_weight.reshape(3, 9 * in_channels, out_channels)
    padded = jnp.pad(volume, ((1, 1), (1, 1), (1, 1), (0, 0)))
    patches, preact = forward_terms(padded, low_three, planes, plane_width)
    preact = preact + bias
    grad_pre = (spread_cotangent(cotangent, planes, plane_width, out_channels) * 0.125 * gelu_slope(preact)).astype(jnp.bfloat16)
    weight_grad = scaling * weight_terms(patches, grad_pre, planes, plane_width, in_channels)
    bias_grad = lax.optimization_barrier(jnp.sum(grad_pre.astype(jnp.float32), axis=0))
    grad_pad = jnp.pad(grad_pre.reshape(planes, plane_width, plane_width, out_channels), ((1, 1), (1, 1), (1, 1), (0, 0)))
    input_grad = input_terms(grad_pad, low_weight, planes, plane_width).astype(jnp.bfloat16)
    input_grad = input_grad.reshape(planes, plane_width, plane_width, in_channels)
    return (weight - learning_rate * weight_grad, bias - learning_rate * bias_grad, input_grad)

def reference(volume, cotangent, weight, bias, exponent):
    updated, updated_bias, input_grad = lax.map(replica_step, (volume, cotangent, weight, bias))
    replicas = weight.shape[0]
    indices = jnp.arange(replicas, dtype=jnp.int32)
    for round_index in range(exponent.shape[0]):
        partner = jnp.bitwise_xor(indices, jnp.left_shift(jnp.int32(1), exponent[round_index].astype(jnp.int32)))
        updated = 0.5 * (updated + jnp.take(updated, partner, axis=0))
        updated_bias = 0.5 * (updated_bias + jnp.take(updated_bias, partner, axis=0))
    return (updated, updated_bias, input_grad)
```

```python
from functools import partial
import math

import jax
import jax.numpy as jnp
from jax import lax
from jax.experimental import pallas as pl
from jax.experimental.pallas import tpu as pltpu
from jax.sharding import PartitionSpec as P

learning_rate = 0.5
cubic = 0.044715
f32 = jnp.float32
bf16 = jnp.bfloat16
VMEM = pl.BlockSpec(memory_space=pltpu.VMEM)
SMEM = pl.BlockSpec(memory_space=pltpu.SMEM)
ANY = pl.BlockSpec(memory_space=pl.ANY)


def gelu_slope(values):
    factor = math.sqrt(2.0 / math.pi)
    inner_arg = factor * (values + cubic * values * values * values)
    tangent = jnp.tanh(inner_arg)
    return 0.5 * (1.0 + tangent) + 0.5 * values * (1.0 - tangent * tangent) * factor * (
        1.0 + 3.0 * cubic * values * values
    )


def col_shifts(flat, width):
    cells = flat.shape[0]
    wide = flat.astype(f32)
    col = lax.broadcasted_iota(jnp.int32, flat.shape, 0) % width
    before = jnp.where(col == 0, 0.0, pltpu.roll(wide, 1, 0)).astype(flat.dtype)
    after = jnp.where(col == width - 1, 0.0, pltpu.roll(wide, cells - 1, 0)).astype(flat.dtype)
    return before, after


def fill_shifted(dst, plane, left, mid, right):
    rows, width = dst.shape[1] - 2, dst.shape[2]
    chans = mid.shape[1]
    blank = jnp.zeros((1, width, 3 * chans), dst.dtype)
    dst[plane, 0:1] = blank
    dst[plane, rows + 1 : rows + 2] = blank
    for c, part in enumerate((left, mid, right)):
        dst[plane, 1 : rows + 1, :, c * chans : (c + 1) * chans] = part.reshape(rows, width, chans)


def row_dot(src, plane, row, step, weights, flip=False):
    width = src.shape[2]
    parts = [
        src[plane, pl.ds(row + (2 - b if flip else b), step)].reshape(step * width, src.shape[3])
        for b in range(3)
    ]
    lhs = jnp.concatenate(parts, axis=1)
    dims = (((1,), (0,)), ((), ()))
    return lax.dot_general(lhs, weights, dims, preferred_element_type=f32)


def prep_kernel(scaling, step, vol, weight, cot, xs, low, pre, cup):
    planes, rows, width, chans = vol.shape
    half = cot.shape[0]
    for plane in range(planes):
        flat = vol[plane].reshape(rows * width, chans)
        before, after = col_shifts(flat, width)
        fill_shifted(xs, plane, before, flat, after)
    low[...] = (scaling * weight[...]).astype(bf16)
    small = cot.shape[1] * half
    tall = half * width
    row = lax.broadcasted_iota(jnp.int32, (tall, small), 0)
    col = lax.broadcasted_iota(jnp.int32, (tall, small), 1)
    pick = (row // width) * cot.shape[1] + (row % width) // 2 == col
    wide = lax.dot_general(
        pick.astype(f32).astype(bf16), cot[...].reshape(small, cot.shape[2]),
        (((1,), (0,)), ((), ())), preferred_element_type=f32,
    )
    cup[...] = wide.reshape(half, width, cot.shape[2]).astype(bf16)
    taps, _, outs = low.shape
    for plane in range(planes):
        for block in range(rows // step):
            total = None
            for a in range(3):
                source = plane + a - 1
                if source < 0 or source >= planes:
                    continue
                part = row_dot(
                    xs, source, block * step, step, low[9 * a : 9 * a + 9].reshape(9 * chans, outs)
                )
                total = part if total is None else total + part
            pre[plane, pl.ds(block * step, step)] = total.reshape(step, width, outs)


def main_kernel(
    scaling, gz, step, split, ids, lo, hi, xs, low, pre, cup, bias, weight,
    send_a, top_a, keep_a, send_b, top_b, keep_b, grad, xh, tiles,
):
    planes, rows, width, outs = pre.shape
    chans = weight.shape[1]
    for side, ref in enumerate((lo, hi)):
        flat = ref[...].reshape(rows * width, chans)
        flat = jnp.where(ids[2 + side] == 0, jnp.zeros_like(flat), flat)
        before, after = col_shifts(flat, width)
        fill_shifted(xh, side, before, flat, after)
    sums = jnp.zeros((1, outs), f32)
    for plane in range(planes):
        for block in range(rows // step):
            span = pl.ds(block * step, step)
            total = pre[plane, span].reshape(step * width, outs) + bias[...]
            if plane == 0:
                total += row_dot(xh, 0, block * step, step, low[0:9].reshape(9 * chans, outs))
            if plane == planes - 1:
                total += row_dot(xh, 1, block * step, step, low[18:27].reshape(9 * chans, outs))
            slope = gelu_slope(total).reshape(step, width, outs)
            got = []
            for pair in range(step // 2):
                up = cup[(plane // 2) * (rows // 2) + block * (step // 2) + pair].astype(f32) * 0.125
                for inner in range(2):
                    got.append((up * slope[2 * pair + inner]).astype(bf16)[None])
            block_grad = jnp.concatenate(got, axis=0)
            grad[plane, span] = block_grad
            flat = block_grad.reshape(step * width, outs).astype(f32)
            sums += jnp.sum(flat, axis=0, keepdims=True)
    blocks, _, high, lanes = tiles.shape
    halves = outs // lanes

    def emit(tile, slot, which):
        send, top, keep = which
        for index in range(blocks):
            i, h = divmod(index, halves)
            tiles[index, 0] = tile[i * high : (i + 1) * high, h * lanes : (h + 1) * lanes].astype(bf16)
        me = ids[0] if send is send_a else ids[1]
        for rel in range(blocks):
            value = tiles[lax.bitwise_xor(me, rel), 0]
            if rel >= blocks // 2:
                send[rel - blocks // 2, slot] = value
            elif rel >= blocks // 4:
                top[rel - blocks // 4, slot] = value
            else:
                keep[rel, slot] = value

    first = (send_a, top_a, keep_a)
    second = (send_b, top_b, keep_b)
    for group in range(9):
        a, b = divmod(group, 3)
        total = None
        for plane in range(planes):
            source = plane + a - 1
            if source < 0:
                lhs = xh[0, b : b + rows]
            elif source >= planes:
                lhs = xh[1, b : b + rows]
            else:
                lhs = xs[source, b : b + rows]
            part = lax.dot_general(
                lhs.reshape(rows * width, 3 * chans), grad[plane].reshape(rows * width, outs),
                (((0,), (0,)), ((), ())), preferred_element_type=f32,
            )
            total = part if total is None else total + part
        for c in range(3):
            tap = 3 * group + c
            tile = (1.0 / gz) * weight[tap] - (learning_rate * scaling) * total[c * chans : (c + 1) * chans]
            if tap < split:
                emit(tile, tap, first)
            else:
                emit(tile, tap - split, second)
    tile = (1.0 / gz) * bias[...] - learning_rate * sums
    emit(jnp.broadcast_to(tile, (chans, outs)), weight.shape[0] - split, second)


def input_kernel(step, grad, low, own, below, above, gs, acc, wt):
    planes, rows, width, outs = grad.shape
    chans = low.shape[1]
    for plane in range(planes):
        flat = grad[plane].reshape(rows * width, outs)
        before, after = col_shifts(flat, width)
        fill_shifted(gs, plane, after, flat, before)
    for tap in range(low.shape[0]):
        a, b, c = tap // 9, tap // 3 % 3, tap % 3
        wt[(3 * b + c) * outs : (3 * b + c + 1) * outs, a * chans : (a + 1) * chans] = low[tap].T
    for plane in range(planes):
        for block in range(rows // step):
            span = pl.ds(block * step, step)
            got = row_dot(gs, plane, block * step, step, wt[...], flip=True)
            for a in range(3):
                target = plane + a
                part = got[:, a * chans : (a + 1) * chans].reshape(step, width, chans)
                if target == 0:
                    below[span] = part.astype(bf16)
                elif target == planes + 1:
                    above[span] = part.astype(bf16)
                elif plane == max(0, target - 2):
                    acc[target - 1, span] = part
                else:
                    acc[target - 1, span] = acc[target - 1, span] + part
    own[...] = acc[...]


def final_kernel(split, count, ids, *refs):
    pieces_a, pieces_b = refs[:count], refs[count : 2 * count]
    new_w, new_b, buf, sem = refs[2 * count :]
    taps, chans, outs = buf.shape
    starts = [0]
    for piece in pieces_a:
        starts.append(starts[-1] + piece.shape[0])
    blocks = starts[-1]
    high, lanes = pieces_a[0].shape[2:]
    halves = outs // lanes
    copies = []
    for which, (pieces, begin, end) in enumerate(((pieces_a, 0, split), (pieces_b, split, taps))):
        for k, piece in enumerate(pieces):
            for j in range(piece.shape[0]):
                place = lax.bitwise_xor(ids[which], starts[k] + j)
                i, h = place // halves, place % halves
                buf[
                    begin:end,
                    pl.ds(pl.multiple_of(i * high, high), high),
                    pl.ds(pl.multiple_of(h * lanes, lanes), lanes),
                ] = piece[j, 0 : end - begin].astype(f32)
                if which == 1:
                    @pl.when(i == 0)
                    def _():
                        new_b[:, pl.ds(pl.multiple_of(h * lanes, lanes), lanes)] = (
                            piece[j, end - begin, 0:1].astype(f32)
                        )
        copy = pltpu.make_async_copy(buf.at[begin:end], new_w.at[begin:end], sem.at[which])
        copy.start()
        copies.append(copy)
    for copy in copies:
        copy.wait()


def swap(block, axis, mask):
    count = lax.axis_size(axis)
    return lax.ppermute(block, axis, [(i, i ^ mask) for i in range(count)])


def total_of(left, right):
    return (left.astype(f32) + right.astype(f32)).astype(bf16)


def per_device(volume, cotangent, weight, bias, exponent):
    vol, cot, master = volume[0], cotangent[0], weight[0]
    planes, rows, width, chans = vol.shape
    taps, _, outs = master.shape
    scaling = (taps * chans) ** (-0.5)
    gz, dp = lax.axis_size("gz"), lax.axis_size("dp")
    gz_bits, dp_bits = gz.bit_length() - 1, dp.bit_length() - 1
    zi, di = lax.axis_index("gz"), lax.axis_index("dp")
    split = 15
    step = 8
    lanes = 128
    blocks = 4 * gz
    halves = outs // lanes
    high = chans * halves // blocks
    slots = (split, taps - split + 1)
    low_bit, high_bit = di & 1, di >> (dp_bits - 1)
    path_a = [("dp", 1), ("dp", dp // 2)] + [("gz", 1 << k) for k in range(gz_bits)]
    path_b = [("dp", 1), ("gz", 1), ("dp", dp // 2)] + [("gz", 1 << k) for k in range(1, gz_bits)]

    def number(path):
        value = 0
        for axis, mask in path:
            bit = ((di if axis == "dp" else zi) & mask) // mask
            value = value * 2 + bit
        return value.astype(jnp.int32)

    me_a, me_b = number(path_a), number(path_b)
    ids = jnp.stack([me_a, me_b, (zi > 0).astype(jnp.int32), (zi < gz - 1).astype(jnp.int32)])

    even = (zi & 1) == 0
    inner = []
    for low_z in range(1, gz - 1, 2):
        inner += [(low_z, low_z + 1), (low_z + 1, low_z)]

    def trade(first, last):
        paired = swap(jnp.where(even, last, first), "gz", 1)
        other = lax.ppermute(jnp.where(even, first, last), "gz", inner)
        return jnp.where(even, other, paired), jnp.where(even, paired, other)

    below, above = trade(vol[0], vol[planes - 1])
    sds = jax.ShapeDtypeStruct
    params = pltpu.CompilerParams(vmem_limit_bytes=60 * 1024 * 1024)
    xs, low, pre, cup = pl.pallas_call(
        partial(prep_kernel, scaling, step),
        out_shape=(
            sds((planes, rows + 2, width, 3 * chans), bf16),
            sds((taps, chans, outs), bf16),
            sds((planes, rows, width, outs), f32),
            sds((planes // 2 * rows // 2, width, outs), bf16),
        ),
        in_specs=[VMEM] * 3, out_specs=(VMEM,) * 4, compiler_params=params, name="prep",
    )(vol, master, cot.reshape(planes // 2 * rows // 2, width // 2, outs))

    def parts(slot):
        return tuple(
            sds((n, slot, high, lanes), bf16) for n in (blocks // 2, blocks // 4, blocks // 4)
        )

    got = pl.pallas_call(
        partial(main_kernel, scaling, gz, step, split),
        out_shape=parts(slots[0]) + parts(slots[1]) + (sds((planes, rows, width, outs), bf16),),
        in_specs=[SMEM] + [VMEM] * 8, out_specs=(VMEM,) * 7,
        scratch_shapes=[
            pltpu.VMEM((2, rows + 2, width, 3 * chans), bf16),
            pltpu.VMEM((blocks, 1, high, lanes), bf16),
        ],
        compiler_params=params, name="main",
    )(ids, below, above, xs, low, pre, cup, bias, master)
    triple_a, triple_b, grad = got[:3], got[3:6], got[6]

    hits = [jnp.any(exponent == k) for k in range(dp_bits)]

    def input_part():
        own, to_below, to_above = pl.pallas_call(
            partial(input_kernel, step),
            out_shape=(
                sds((planes, rows, width, chans), f32),
                sds((rows, width, chans), bf16),
                sds((rows, width, chans), bf16),
            ),
            in_specs=[VMEM] * 2, out_specs=(VMEM,) * 3,
            scratch_shapes=[
                pltpu.VMEM((planes, rows + 2, width, 3 * outs), bf16),
                pltpu.VMEM((planes, rows, width, chans), f32),
                pltpu.VMEM((9 * outs, 3 * chans), bf16),
            ],
            compiler_params=params, name="input_grad",
        )(grad, low)
        from_below, from_above = trade(to_below, to_above)
        from_below = jnp.where(zi > 0, from_below, jnp.zeros_like(from_below))
        from_above = jnp.where(zi < gz - 1, from_above, jnp.zeros_like(from_above))
        bottom = (own[0] + from_below.astype(f32)).astype(bf16)
        top = (own[planes - 1] + from_above.astype(f32)).astype(bf16)
        mid = own[1 : planes - 1].astype(bf16)
        return jnp.concatenate([bottom[None], mid, top[None]], axis=0)

    def finish(pieces_a, pieces_b):
        count = len(pieces_a)
        return pl.pallas_call(
            partial(final_kernel, split, count),
            out_shape=(sds((taps, chans, outs), f32), sds((1, outs), f32)),
            in_specs=[SMEM] + [VMEM] * (2 * count), out_specs=(ANY, VMEM),
            scratch_shapes=[pltpu.VMEM((taps, chans, outs), f32), pltpu.SemaphoreType.DMA((2,))],
            compiler_params=params, name="final",
        )(ids, *pieces_a, *pieces_b)

    def averaged(value, middle, scale):
        value = scale * value
        for k in middle:
            other = swap(value.astype(bf16), "dp", 1 << k)
            value = jnp.where(hits[k], 0.5 * (value + other.astype(f32)), value)
        return value

    def paired_path():
        grads = input_part()
        state = []
        for triple, path in ((triple_a, path_a), (triple_b, path_b)):
            send, top, keep = triple
            state.append([send, top, keep])
        after = []
        for send, top, keep in state:
            other = swap(send, "dp", 1)
            after.append((total_of(top, other[blocks // 4 :]), total_of(keep, other[: blocks // 4])))
        width_now = blocks // 4
        held = after
        for level in range(1, len(path_a)):
            nexts = []
            for (send, keep), path in zip(held, (path_a, path_b)):
                other = swap(send, *path[level])
                half = width_now // 2
                if half:
                    nexts.append((total_of(keep[half:], other[half:]), total_of(keep[:half], other[:half])))
                else:
                    nexts.append(keep.astype(f32) + other.astype(f32))
            held, width_now = nexts, width_now // 2
        own = []
        for value in held:
            own.append(averaged(value, range(1, dp_bits - 1), 0.25).astype(bf16))
        gathered = [[value] for value in own]
        for level in range(len(path_a) - 1, 0, -1):
            for pieces, path in zip(gathered, (path_a, path_b)):
                block = pieces[0] if len(pieces) == 1 else jnp.concatenate(pieces, axis=0)
                pieces.append(swap(block, *path[level]))
        whole = []
        for pieces in gathered:
            whole.append(pieces + [swap(piece, "dp", 1) for piece in pieces])
        return finish(*whole) + (grads,)

    def general_path():
        grads = input_part()
        whole = []
        for triple, path in ((triple_a, path_a), (triple_b, path_b)):
            send, top, keep = triple
            value = jnp.concatenate([keep, top, send], axis=0)
            value = value.reshape((2,) * len(path) + value.shape[1:])
            for level, (axis, mask) in enumerate(path):
                if axis == "gz":
                    mine = lax.slice_in_dim(value, 0, 1, axis=level)
                    theirs = lax.slice_in_dim(value, 1, 2, axis=level)
                    value = total_of(mine, swap(theirs, axis, mask))
            value = value.astype(f32)
            for k in range(dp_bits):
                other = swap(value.astype(bf16), "dp", 1 << k).astype(f32)
                if ("dp", 1 << k) in path:
                    other = jnp.flip(other, axis=path.index(("dp", 1 << k)))
                value = jnp.where(hits[k], 0.5 * (value + other), value)
            value = value.astype(bf16)
            for level, (axis, mask) in reversed(list(enumerate(path))):
                if axis == "gz":
                    value = jnp.concatenate([value, swap(value, axis, mask)], axis=level)
            value = value.reshape((blocks,) + value.shape[len(path) :])
            sizes = [1] + [1 << k for k in range(len(path))]
            pieces, begin = [], 0
            for size in sizes:
                pieces.append(value[begin : begin + size])
                begin += size
            half = pieces[:-1]
            other_half, begin = [], 0
            for piece in half:
                other_half.append(pieces[-1][begin : begin + piece.shape[0]])
                begin += piece.shape[0]
            whole.append(half + other_half)
        return finish(*whole) + (grads,)

    both = jnp.logical_and(hits[0], hits[dp_bits - 1])
    new_w, new_b, grads = lax.cond(both, paired_path, general_path)
    return new_w[None], new_b, grads[None]


def solution(mesh):
    in_specs = (
        P("dp", "gz", None, None, None),
        P("dp", "gz", None, None, None),
        P("dp", None, None, None),
        P("dp", None),
        P(),
    )
    out_specs = (P("dp", None, None, None), P("dp", None), P("dp", "gz", None, None, None))
    return jax.shard_map(
        per_device, mesh=mesh, in_specs=in_specs, out_specs=out_specs, check_vma=False
    )
```
